512 devices in a mesh: src: 16 (over x_hi, y, core), rcv: 32 (over z, x_lo).
Axes of the slice: x: 4 (x_hi: 2, x_lo: 2; x = x_hi * 2 + x_lo), y: 4, z: 16, core: 2. Of those that a mesh axis runs over, the one named last changes fastest.
Arguments:
- spectra: bfloat16 [1024, 287, 192], P(('src', 'rcv')), may hold values from -6 to 6
- block_mask: int32 [16, 16], replicated, may hold values from 0 to 1, as said below
Outputs:
- correlations: bfloat16 [1024, 16, 64, 576], P('src', None, 'rcv')
The draws below stay inside these ranges and needn't reach their ends.
Inputs may be any that keep to these rules, and one draw needn't show every extreme that they name: `block_mask`: symmetric, with ones on the diagonal.
All inputs are finite; a program needn't handle non-finite values.
Results may differ from the reference program's by a relative error of at most 0.0055.
Values may be sent and summed in bfloat16 or wider, within the bound.
A program may use at most 128 MiB of HBM per device.

```python
import math
import jax
import jax.numpy as jnp
from jax import lax

BLOCK = 64
BINS = 32
SEGS = 287
BLOCKS = 16
STATIONS = 1024


def draw_block_mask(key, part):
    spots = jax.random.randint(key, (BLOCKS, 2), 0, 12)
    offset = spots[:, None, :] - spots[None, :, :]
    spacing = jnp.sum(offset * offset, axis=2)
    return (spacing <= 20).astype(jnp.int32)


def block_scale(rng, dims, cuts, low, top_value):
    level, own = 1.0, jax.random.fold_in(rng, 6)
    for dim, shards_of in cuts:
        draws = jnp.exp(jax.random.uniform(jax.random.fold_in(own, dim), (shards_of,), jnp.float32, low / len(cuts), top_value / len(cuts)))
        level = level * jnp.repeat(draws, dims[dim] // shards_of).reshape([-1 if axis == dim else 1 for axis in range(len(dims))])
    return level


def noise(rng, extent, spread, bound, split=(), kind=jnp.bfloat16):
    factor_of = block_scale(rng, extent, split, -0.22, 0.18) if split else 1.0
    values = jax.random.normal(rng, extent, jnp.float32) * spread * factor_of
    return jnp.minimum(jnp.maximum(values, -bound), bound).astype(kind)


def setup_inputs(seed: int = 0) -> dict:
    streams_of = jax.random.split(jax.random.key(seed), 3)
    return {
        "spectra": noise(streams_of[0], (STATIONS, SEGS, 6 * BINS), 1.0, 6.0, ((0, 512),)),
        "block_mask": draw_block_mask(jax.random.fold_in(streams_of[2], 71), 0),
    }


def whiten(spectra):
    values = spectra.astype(jnp.float32)
    mean_power = lax.optimization_barrier(jnp.mean(values * values, axis=2, keepdims=True))
    return (values * lax.rsqrt(mean_power + 1e-06)).astype(jnp.bfloat16)

def rotate(right_rows):
    real_part = right_rows[:, :, :, 0]
    imag_part = right_rows[:, :, :, 1]
    as_real = jnp.stack([real_part, imag_part], axis=3)
    as_imag = jnp.stack([-imag_part, real_part], axis=3)
    return jnp.stack([as_real, as_imag], axis=4)

def reference(spectra, block_mask):
    whitened = whiten(spectra).reshape(STATIONS, SEGS, 3, 2, BINS)
    turned = rotate(whitened).astype(jnp.float32)
    norm_scale = 1.0 / math.sqrt(SEGS)
    block_rows = whitened.reshape(BLOCKS, BLOCK, SEGS, 3, 2, BINS)

    def per_block(inputs):
        left_rows, mask_line = inputs
        values = jnp.einsum('iwacf,jwbcef->ijabef', left_rows.astype(jnp.float32), turned, precision=lax.Precision.HIGHEST)
        values = values.reshape(BLOCK, BLOCKS, BLOCK, 18 * BINS) * norm_scale
        values = values * mask_line.astype(jnp.float32)[None, :, None, None]
        return values.astype(jnp.bfloat16)
    result = lax.map(per_block, (block_rows, block_mask))
    return result.reshape(STATIONS, BLOCKS, BLOCK, 18 * BINS)
```

```python
import functools
import math

import jax
import jax.numpy as jnp
import numpy as np
from jax import lax
from jax.experimental import pallas as pl
from jax.experimental.pallas import tpu as pltpu
from jax.sharding import PartitionSpec as P

MESH = pl.DeviceIdType.MESH
F32 = jnp.float32
BF16 = jnp.bfloat16
NT = (((1,), (1,)), ((), ()))


def source_selector():
    table = np.zeros((16, 24, 2, 192), np.float32)
    for fp in range(16):
        for c in range(2):
            for h in range(2):
                for s in range(2):
                    row = c * 4 + h * 2 + s
                    table[fp, row, s, h * 64 + c * 32 + fp] = 1
                    table[fp, 8 + row, s, 2 * 64 + c * 32 + fp + 16 * h] = 1
                    table[fp, 16 + row, s, h * 64 + c * 32 + fp + 16] = 1
    return table.reshape(384, 384)


def receiver_selector():
    table = np.zeros((32, 2, 4, 2, 2, 192), np.float32)
    for f in range(32):
        for c in range(2):
            for b in range(3):
                for s in range(2):
                    table[f, c, b, s, s, b * 64 + c * 32 + f] = 1
    return table.reshape(512, 384)


def output_selector():
    table = np.zeros((3, 16, 2, 16, 4, 2), np.float32)
    for b in range(3):
        for k in range(16):
            for s in range(2):
                table[b, k, s, k, b, s] = 1
    return table.reshape(96, 128)


def arrange(w_ref, ga_ref, gb_ref, qa_ref, qb_ref):
    ga, gb = ga_ref[...], gb_ref[...]
    w = jnp.concatenate([w_ref[0], w_ref[1]], axis=1)
    ya = lax.dot_general(ga, w, NT, preferred_element_type=F32).astype(BF16)
    yb = lax.dot_general(gb, w, NT, preferred_element_type=F32).astype(BF16)
    for kt in range(2):
        qa_ref[kt * 16 : kt * 16 + 16] = ya[:, kt * 128 : kt * 128 + 128].reshape(16, 24, 128)
        qb_ref[kt * 64 : kt * 64 + 64] = yb[:, kt * 128 : kt * 128 + 128].reshape(64, 8, 128)
    rest = w[256:288]
    ga4 = ga.reshape(4, 4, 24, 384)
    gb4 = gb.reshape(8, 4, 16, 384)
    ta = jnp.zeros((96, 128), F32)
    tb = jnp.zeros((128, 128), F32)
    for q in range(4):
        parts = [rest if p == q else jnp.zeros_like(rest) for p in range(4)]
        placed = jnp.concatenate(parts, axis=0)
        ta += lax.dot_general(ga4[:, q].reshape(96, 384), placed, NT, preferred_element_type=F32)
        tb += lax.dot_general(gb4[:, q].reshape(128, 384), placed, NT, preferred_element_type=F32)
    qa_ref[32:36] = ta.astype(BF16).reshape(4, 24, 128)
    qb_ref[128:144] = tb.astype(BF16).reshape(16, 8, 128)


def gather(nx, qa, qb, a_out, b_out, sems_own, sems_par, sems_x, sems_b, s_own, s_par, s_x, s_b, loc):
    src, rcv = lax.axis_index("src"), lax.axis_index("rcv")
    z, p = rcv // 2, rcv % 2
    col = 1 - p
    y = (src // 2) % 4
    hi, low = src // 8, src % 2
    up = (src, ((z + 1) % 16) * 2 + p)
    down = (src, ((z + 15) % 16) * 2 + p)
    side = (src, z * 2 + col)
    far = ((src + 8) % 16, rcv)
    twin = (src - low + (1 - low), rcv)
    ys = [(hi * 8 + ((y + d) % 4) * 2 + low, rcv) for d in (1, 3, 2)]
    peers = [up, down, side, far, twin] + ys

    barrier = pltpu.get_barrier_semaphore()
    for peer in peers:
        pl.semaphore_signal(barrier, inc=1, device_id=peer, device_id_type=MESH)
    pl.semaphore_wait(barrier, len(peers))

    def remote(source, target, send, recv, peer):
        return pltpu.make_async_remote_copy(
            src_ref=source, dst_ref=target, send_sem=send, recv_sem=recv, device_id=peer, device_id_type=MESH
        )

    def wholes(ref, zz, pp):
        return ref.at[zz * 2 + pp]

    def parts(ref, zz, pp, lo, hi_):
        return ref.at[zz * 2 + pp, pl.ds(lo, hi_ - lo)]

    def b_slot(i):
        return b_out.at[:, pl.ds(pl.multiple_of(i * 8, 8), 8)]

    first = [
        remote(qa, wholes(a_out, z, p), s_own.at[0, 0], sems_own.at[0, 0], up),
        remote(qa, wholes(a_out, z, p), s_own.at[1, 0], sems_own.at[1, 0], down),
        remote(qa, wholes(a_out, z, p), s_x.at[0], sems_x.at[0], side),
        remote(qb, b_slot(src), s_b.at[0], sems_b.at[src], far),
        remote(qb, b_slot(src), s_b.at[1], sems_b.at[src], ys[0]),
        remote(qb, b_slot(src), s_b.at[2], sems_b.at[src], ys[1]),
        remote(qb, b_slot(src), s_b.at[3], sems_b.at[src], ys[2]),
        remote(qb, b_slot(src), s_b.at[4], sems_b.at[src], twin),
    ]
    for copy in first:
        copy.start()
    own_a = pltpu.make_async_copy(qa, wholes(a_out, z, p), loc.at[0])
    own_b = pltpu.make_async_copy(qb, b_slot(src), loc.at[1])
    own_a.start()
    own_b.start()
    remote(qa, wholes(a_out, z, col), s_x.at[0], sems_x.at[0], side).wait_recv()
    par0 = [
        remote(parts(a_out, z, col, nx, 36), parts(a_out, z, col, nx, 36), s_par.at[0, 0], sems_par.at[0, 0], up),
        remote(parts(a_out, z, col, nx, 36), parts(a_out, z, col, nx, 36), s_par.at[1, 0], sems_par.at[1, 0], down),
    ]
    for copy in par0:
        copy.start()

    half = 18
    halfp = nx + (36 - nx) // 2

    def piece_b(i, send, peer):
        return remote(b_slot(i), b_slot(i), s_b.at[send], sems_b.at[i], peer)

    far_i = (src + 8) % 16
    y_is = [ys[0][0], ys[1][0], ys[2][0]]
    f_is = [(i + 8) % 16 for i in y_is]
    low_of = src - low + (1 - low)

    def b_wait(i):
        remote(b_slot(i), b_slot(i), s_b.at[0], sems_b.at[i], far).wait_recv()

    def ring(t, carry):
        zu, zd = (z + 16 - t) % 16, (z + t) % 16
        for way, zz, peer in ((0, zu, up), (1, zd, down)):
            slot = wholes(a_out, zz, p)
            remote(slot, slot, s_own.at[way, t - 1], sems_own.at[way, t - 1], peer).wait_recv()
            remote(slot, slot, s_own.at[way, t], sems_own.at[way, t], peer).start()
            if nx:
                xs = parts(a_out, zz, p, 0, nx)
                remote(xs, xs, s_x.at[2 * t - 1 + way], sems_x.at[2 * t - 1 + way], side).start()
        for way, zz, peer in ((0, zu, up), (1, zd, down)):
            slot = parts(a_out, zz, col, nx, 36)
            remote(slot, slot, s_par.at[way, t - 1], sems_par.at[way, t - 1], peer).wait_recv()
            remote(slot, slot, s_par.at[way, t], sems_par.at[way, t], peer).start()
        return carry

    lax.fori_loop(1, 2, ring, 0)
    b_wait(far_i)
    for k in range(3):
        piece_b(far_i, 5 + k, ys[k]).start()
    piece_b(far_i, 8, twin).start()
    lax.fori_loop(2, 4, ring, 0)
    for k in range(3):
        b_wait(y_is[k])
        piece_b(y_is[k], 9 + k, twin).start()
    lax.fori_loop(4, 6, ring, 0)
    for k in range(3):
        b_wait(f_is[k])
        piece_b(f_is[k], 12 + k, twin).start()
    lax.fori_loop(6, 7, ring, 0)
    z8 = (z + 8) % 16
    for way, zz, peer in ((0, (z + 9) % 16, up), (1, (z + 7) % 16, down)):
        slot = wholes(a_out, zz, p)
        remote(slot, slot, s_own.at[way, 6], sems_own.at[way, 6], peer).wait_recv()
        piece = parts(a_out, zz, p, 0, half) if way == 0 else parts(a_out, zz, p, half, 36)
        remote(piece, piece, s_own.at[way, 7], sems_own.at[way, 7], peer).start()
        if nx:
            xs = parts(a_out, zz, p, 0, nx)
            remote(xs, xs, s_x.at[13 + way], sems_x.at[13 + way], side).start()
    for way, zz, peer in ((0, (z + 9) % 16, up), (1, (z + 7) % 16, down)):
        slot = parts(a_out, zz, col, nx, 36)
        remote(slot, slot, s_par.at[way, 6], sems_par.at[way, 6], peer).wait_recv()
        piece = parts(a_out, zz, col, nx, halfp) if way == 0 else parts(a_out, zz, col, halfp, 36)
        remote(piece, piece, s_par.at[way, 7], sems_par.at[way, 7], peer).start()
    for way, peer in ((0, up), (1, down)):
        piece = parts(a_out, z8, p, 0, half) if way == 0 else parts(a_out, z8, p, half, 36)
        remote(piece, piece, s_own.at[way, 7], sems_own.at[way, 7], peer).wait_recv()
    if nx:
        xs = parts(a_out, z8, p, 0, nx)
        remote(xs, xs, s_x.at[15], sems_x.at[15], side).start()
    for way, peer in ((0, up), (1, down)):
        piece = parts(a_out, z8, col, nx, halfp) if way == 0 else parts(a_out, z8, col, halfp, 36)
        remote(piece, piece, s_par.at[way, 7], sems_par.at[way, 7], peer).wait_recv()
    if nx:
        def side_wait(k, carry):
            t = (k + 1) // 2
            zz = (z + (16 - t) * (k % 2) + t * (1 - k % 2)) % 16
            xs = parts(a_out, zz, col, 0, nx)
            remote(xs, xs, s_x.at[k], sems_x.at[k], side).wait_recv()
            return carry

        lax.fori_loop(1, 16, side_wait, 0)
    for i in [low_of, (low_of + 8) % 16]:
        b_wait(i)
    for k in range(3):
        b_wait(y_is[k] - low + (1 - low))
        b_wait(f_is[k] - low + (1 - low))
    own_a.wait()
    own_b.wait()

    def sent(t, carry):
        for way, peer in ((0, up), (1, down)):
            slot = wholes(a_out, z, p)
            remote(slot, slot, s_own.at[way, t], sems_own.at[way, t], peer).wait_send()
            slot = parts(a_out, z, col, nx, 36)
            remote(slot, slot, s_par.at[way, t], sems_par.at[way, t], peer).wait_send()
        return carry

    lax.fori_loop(0, 7, sent, 0)
    for way, peer in ((0, up), (1, down)):
        piece = parts(a_out, z, p, 0, half) if way == 0 else parts(a_out, z, p, half, 36)
        remote(piece, piece, s_own.at[way, 7], sems_own.at[way, 7], peer).wait_send()
        piece = parts(a_out, z, col, nx, halfp) if way == 0 else parts(a_out, z, col, halfp, 36)
        remote(piece, piece, s_par.at[way, 7], sems_par.at[way, 7], peer).wait_send()
    remote(qa, wholes(a_out, z, p), s_x.at[0], sems_x.at[0], side).wait_send()
    if nx:
        def side_sent(k, carry):
            xs = parts(a_out, z, p, 0, nx)
            remote(xs, xs, s_x.at[k], sems_x.at[k], side).wait_send()
            return carry

        lax.fori_loop(1, 16, side_sent, 0)

    def b_sent(k, carry):
        remote(qb, b_slot(src), s_b.at[k], sems_b.at[src], far).wait_send()
        return carry

    lax.fori_loop(0, 15, b_sent, 0)


def cross(a0, a1, a2, b00, b01, b02, b10, b11, b12, wt_ref, l_ref, out_ref, u_ref):
    step = pl.program_id(0)

    @pl.when(step < 16)
    def _():
        q = step % 4
        lane = lax.broadcasted_iota(jnp.int32, (1, 128), 1) // 32
        keep = (lane == q).astype(BF16)
        wt = wt_ref[...]
        sign = jnp.where(lax.broadcasted_iota(jnp.int32, (8, 128), 0) < 4, 1.0, -1.0)
        wq = (wt * sign)[None]
        for h, bs in ((0, (b00, b01, b02)), (1, (b10, b11, b12))):
            lhs = jnp.concatenate(
                [r[:, 0, 8 * h : 8 * h + 16, :].reshape(512, 128) for r in (a0, a1, a2)], axis=1
            )
            rhs = jnp.concatenate(
                [bs[0][...].reshape(256, 128), bs[1][...].reshape(256, 128), bs[2][...].reshape(256, 128) * keep],
                axis=1,
            )
            r = lax.dot_general(lhs, rhs, NT, preferred_element_type=F32)
            pr = r[:, :128].reshape(64, 8, 128)
            qr = r[:, 128:].reshape(64, 8, 128)
            u = pr * wt[None] + pltpu.roll(qr, 4, 1) * wq
            u_ref[pl.ds(pl.multiple_of((step + 16 * h) * 512, 512), 512), :] = u.reshape(512, 128)

    @pl.when(step >= 16)
    def _():
        sel = l_ref[...]
        low = lax.broadcasted_iota(jnp.int32, (32, 128), 1) < 64
        for i8 in range(8):
            i = (step - 16) * 8 + i8
            base = (i // 2) * 16 + i % 2
            rows = []
            for a in range(3):
                for e in range(2):
                    r0 = (0, 2, 8)[a] + e * 4
                    r1 = (8, 10, 2)[a] + e * 4
                    rows.append(u_ref[pl.ds(base + r0, 16, stride=512), :])
                    rows.append(u_ref[pl.ds(16 * 512 + base + r1, 16, stride=512), :])
            xa = [jnp.concatenate(rows[4 * a : 4 * a + 4], axis=0).astype(BF16) for a in range(3)]
            rhs = jnp.concatenate([xa[0], xa[1], xa[1], xa[0], xa[2], xa[2]], axis=0)
            c = lax.dot_general(sel, rhs, NT, preferred_element_type=F32)
            t1, t2, t3 = c[:, :128], c[:, 128:256], c[:, 256:]
            b = lambda m, k: m[32 * k : 32 * k + 32]
            tiles = [
                jnp.where(low, b(t1, 0), b(t2, 1)),
                jnp.where(low, b(t1, 2), b(t1, 0)),
                jnp.where(low, b(t2, 1), b(t1, 2)),
                jnp.where(low, b(t3, 0), b(t3, 1)),
                b(t3, 2)[:, :64],
            ]
            out_ref[i8] = jnp.concatenate(tiles, axis=1).astype(BF16)


def whiten(spectra):
    values = spectra.astype(F32)
    mean_power = jnp.mean(values * values, axis=2, keepdims=True)
    return (values * lax.rsqrt(mean_power + 1e-06)).astype(BF16)


NX = 20


def on_device(spectra, block_mask):
    segs = spectra.shape[1]
    scale = 1.0 / math.sqrt(segs)
    w = jnp.pad(whiten(spectra), ((0, 0), (0, 288 - segs), (0, 0)))
    ga, gb = jnp.asarray(source_selector(), BF16), jnp.asarray(receiver_selector(), BF16)
    vmem = pl.BlockSpec(memory_space=pltpu.VMEM)
    qa, qb = pl.pallas_call(
        arrange,
        out_shape=(jax.ShapeDtypeStruct((36, 24, 128), BF16), jax.ShapeDtypeStruct((144, 8, 128), BF16)),
        in_specs=[vmem] * 3,
        out_specs=[vmem] * 2,
        name="arrange",
    )(w, ga, gb)
    a, b = comm(qa, qb)
    mask_line = lax.dynamic_index_in_dim(block_mask, lax.axis_index("src"), 0, keepdims=False)
    weights = jnp.where(jnp.arange(8) < 6, scale, 0.0)[None, :] * mask_line.astype(F32)[:, None]
    weights = weights.reshape(1, 128)
    return compute(a, b, weights)


def comm(qa, qb):
    anyspace = pl.BlockSpec(memory_space=pl.ANY)
    dma = pltpu.SemaphoreType.DMA
    return pl.pallas_call(
        functools.partial(gather, NX),
        out_shape=(jax.ShapeDtypeStruct((32, 36, 24, 128), BF16), jax.ShapeDtypeStruct((144, 128, 128), BF16)),
        in_specs=[anyspace] * 2,
        out_specs=[anyspace] * 2,
        scratch_shapes=[
            dma((2, 8)), dma((2, 8)), dma((16,)), dma((16,)),
            dma((2, 8)), dma((2, 8)), dma((16,)), dma((16,)), dma((2,)),
        ],
        compiler_params=pltpu.CompilerParams(collective_id=0, has_side_effects=True),
        name="gather",
    )(qa, qb)


def compute(a, b, weights):
    sel = jnp.asarray(output_selector(), BF16)
    fp = lambda i: jnp.minimum(i, 15)
    a_spec = lambda at: pl.BlockSpec((32, 1, 24, 128), lambda i: (0, at(fp(i)), 0, 0))
    b_spec = lambda at: pl.BlockSpec((2, 128, 128), lambda i: (at(fp(i)), 0, 0))
    out = pl.pallas_call(
        cross,
        grid=(24,),
        out_shape=jax.ShapeDtypeStruct((64, 32, 576), BF16),
        in_specs=[
            a_spec(lambda f: f), a_spec(lambda f: 16 + f), a_spec(lambda f: 32 + f // 4),
            b_spec(lambda f: f), b_spec(lambda f: 32 + f), b_spec(lambda f: 64 + f // 4),
            b_spec(lambda f: 16 + f), b_spec(lambda f: 48 + f), b_spec(lambda f: 68 + f // 4),
            pl.BlockSpec((1, 128), lambda i: (0, 0)),
            pl.BlockSpec((96, 128), lambda i: (0, 0)),
        ],
        out_specs=pl.BlockSpec((8, 32, 576), lambda i: (jnp.maximum(i - 16, 0), 0, 0)),
        scratch_shapes=[pltpu.VMEM((32 * 512, 128), F32)],
        name="cross",
    )(a, a, a, b, b, b, b, b, b, weights, sel)
    return out.reshape(64, 16, 2, 576)


def solution(mesh):
    return jax.shard_map(
        on_device,
        mesh=mesh,
        in_specs=(P(("src", "rcv"), None, None), P()),
        out_specs=P("src", None, "rcv", None),
        check_vma=False,
    )
```

```python
import functools
import math

import jax
import jax.numpy as jnp
import numpy as np
from jax import lax
from jax.experimental import pallas as pl
from jax.experimental.pallas import tpu as pltpu
from jax.sharding import PartitionSpec as P

MESH = pl.DeviceIdType.MESH
F32 = jnp.float32
BF16 = jnp.bfloat16
NT = (((1,), (1,)), ((), ()))


def source_selector():
    table = np.zeros((16, 24, 2, 192), np.float32)
    for fp in range(16):
        for c in range(2):
            for h in range(2):
                for s in range(2):
                    row = c * 4 + h * 2 + s
                    table[fp, row, s, h * 64 + c * 32 + fp] = 1
                    table[fp, 8 + row, s, 2 * 64 + c * 32 + fp + 16 * h] = 1
                    table[fp, 16 + row, s, h * 64 + c * 32 + fp + 16] = 1
    return table.reshape(384, 384)


def receiver_selector():
    table = np.zeros((32, 2, 4, 2, 2, 192), np.float32)
    for f in range(32):
        for c in range(2):
            for b in range(3):
                for s in range(2):
                    table[f, c, b, s, s, b * 64 + c * 32 + f] = 1
    return table.reshape(512, 384)


def output_selector():
    table = np.zeros((3, 16, 2, 16, 4, 2), np.float32)
    for b in range(3):
        for k in range(16):
            for s in range(2):
                table[b, k, s, k, b, s] = 1
    return table.reshape(96, 128)


def arrange(x_ref, ga_ref, gb_ref, qa_ref, qb_ref):
    segs = x_ref.shape[0]
    values = x_ref[...].astype(F32)
    mean_power = jnp.mean(values * values, axis=2, keepdims=True)
    white = (values * lax.rsqrt(mean_power + 1e-06))
    w = jnp.concatenate([white[:, 0, :], white[:, 1, :]], axis=1)
    w = jnp.concatenate([w, jnp.zeros((288 - segs, 384), F32)], axis=0).astype(BF16)
    ga, gb = ga_ref[...], gb_ref[...]
    ya = lax.dot_general(ga, w, NT, preferred_element_type=F32).astype(BF16)
    yb = lax.dot_general(gb, w, NT, preferred_element_type=F32).astype(BF16)
    for kt in range(2):
        qa_ref[kt * 16 : kt * 16 + 16] = ya[:, kt * 128 : kt * 128 + 128].reshape(16, 24, 128)
        qb_ref[kt * 64 : kt * 64 + 64] = yb[:, kt * 128 : kt * 128 + 128].reshape(64, 8, 128)
    rest = w[256:288]
    ga4 = ga.reshape(4, 4, 24, 384)
    gb4 = gb.reshape(8, 4, 16, 384)
    ta = jnp.zeros((96, 128), F32)
    tb = jnp.zeros((128, 128), F32)
    for q in range(4):
        parts = [rest if p == q else jnp.zeros_like(rest) for p in range(4)]
        placed = jnp.concatenate(parts, axis=0)
        ta += lax.dot_general(ga4[:, q].reshape(96, 384), placed, NT, preferred_element_type=F32)
        tb += lax.dot_general(gb4[:, q].reshape(128, 384), placed, NT, preferred_element_type=F32)
    qa_ref[32:36] = ta.astype(BF16).reshape(4, 24, 128)
    qb_ref[128:144] = tb.astype(BF16).reshape(16, 8, 128)


OWN = ((0, 10), (10, 20), (20, 36))
PAR = ((20, 28), (28, 36))
SIDE = OWN[:2]
HALVES = ((0, 72), (72, 144))


def fused(scale, qa, qb, mask_ref, l_ref, out_ref, a_all, b_all, relay, u_ref,
          so, ro, sp, rp, sx, rx, sb, rb, rr, loc):
    src, rcv = lax.axis_index("src"), lax.axis_index("rcv")
    z, p = rcv // 2, rcv % 2
    col = 1 - p
    y = (src // 2) % 4
    hi, low = src // 8, src % 2
    far_i = (src + 8) % 16
    twin_i = src - low + (1 - low)
    up = (src, ((z + 1) % 16) * 2 + p)
    down = (src, ((z + 15) % 16) * 2 + p)
    side = (src, z * 2 + col)
    cross_x = (far_i, z * 2 + col)
    twin = (twin_i, rcv)

    def y_of(base, d):
        return (base // 8) * 8 + ((y + d) % 4) * 2 + low

    yup, ydown = (y_of(src, 1), rcv), (y_of(src, 3), rcv)
    peers = [up, down, side, cross_x, twin, yup, ydown]

    barrier = pltpu.get_barrier_semaphore()
    for peer in peers:
        pl.semaphore_signal(barrier, inc=1, device_id=peer, device_id_type=MESH)
    pl.semaphore_wait(barrier, len(peers))

    def remote(source, target, send, recv, peer):
        return pltpu.make_async_remote_copy(
            src_ref=source, dst_ref=target, send_sem=send, recv_sem=recv, device_id=peer, device_id_type=MESH
        )

    ways = ((0, up), (1, down))

    def units(zz, pp, span):
        return a_all.at[zz * 2 + pp, pl.ds(span[0], span[1] - span[0])]

    def own(zz, t, way, c, source=None):
        slot = units(zz, p, OWN[c])
        return remote(slot if source is None else source, slot, so.at[way, t, c], ro.at[way, t, c], ways[way][1])

    def par(zz, t, way, c):
        slot = units(zz, col, PAR[c])
        return remote(slot, slot, sp.at[way, t, c], rp.at[way, t, c], ways[way][1])

    def side_send(zz, k, c):
        slot = units(zz, p, SIDE[c])
        return remote(slot, slot, sx.at[k, c], rx.at[k, c], side)

    def side_recv(k):
        t = (k + 1) // 2
        zz = (z + (16 - t) * (k % 2) + t * (1 - k % 2)) % 16
        for c in range(2):
            slot = units(zz, col, SIDE[c])
            remote(slot, slot, sx.at[k, c], rx.at[k, c], side).wait_recv()

    b_sent = []

    def b_slot(i, c):
        lo, hi_ = HALVES[c]
        return b_all.at[pl.ds(lo, hi_ - lo), pl.ds(pl.multiple_of(i * 8, 8), 8)]

    def b_own(c):
        return qb.at[pl.ds(HALVES[c][0], HALVES[c][1] - HALVES[c][0])]

    def b_relay(c):
        return relay.at[pl.ds(HALVES[c][0], HALVES[c][1] - HALVES[c][0])]

    def b_start(source, target, recv, peer):
        copy = remote(source, target, sb.at[len(b_sent)], recv, peer)
        copy.start()
        b_sent.append(copy)

    def b_pass(i, c, peer):
        b_start(b_slot(i, c), b_slot(i, c), rb.at[i, c], peer)

    def b_wait(i, c):
        remote(b_slot(i, c), b_slot(i, c), sb.at[0], rb.at[i, c], twin).wait_recv()

    for c in range(2):
        b_start(b_own(c), b_relay(c), rr.at[c], cross_x)
        b_start(b_own(c), b_slot(src, c), rb.at[src, c], yup)
        b_start(b_own(c), b_slot(src, c), rb.at[src, c], ydown)
    for c in range(3):
        span = pl.ds(OWN[c][0], OWN[c][1] - OWN[c][0])
        for way in range(2):
            own(z, 0, way, c, qa.at[span]).start()
    side_first = []
    for c in (2, 0, 1):
        span = pl.ds(OWN[c][0], OWN[c][1] - OWN[c][0])
        slot = units(z, p, OWN[c])
        sem = (0, c) if c < 2 else (16, 0)
        side_first.append(remote(qa.at[span], slot, sx.at[sem], rx.at[sem], side))
    for copy in side_first:
        copy.start()
    for c in range(2):
        b_start(b_own(c), b_slot(src, c), rb.at[src, c], twin)
    local = [
        pltpu.make_async_copy(qa, a_all.at[z * 2 + p], loc.at[0]),
        pltpu.make_async_copy(qb, b_all.at[:, pl.ds(pl.multiple_of(src * 8, 8), 8)], loc.at[1]),
    ]
    for copy in local:
        copy.start()

    row = mask_ref[pl.ds(src, 1), :].astype(F32).astype(BF16)
    spread = lax.broadcasted_iota(jnp.int32, (16, 128), 1) // 8 == lax.broadcasted_iota(jnp.int32, (16, 128), 0)
    lanes = lax.broadcasted_iota(jnp.int32, (1, 128), 1)
    wt = jnp.dot(row, spread.astype(F32).astype(BF16), preferred_element_type=F32)
    wt = wt * jnp.where(lanes % 8 < 6, scale, 0.0)
    sign = jnp.where(lax.broadcasted_iota(jnp.int32, (8, 128), 0) < 4, 1.0, -1.0)
    wq = (wt * sign)[None]

    slot = units(z, col, OWN[2])
    remote(slot, slot, sx.at[16, 0], rx.at[16, 0], side).wait_recv()
    for c in range(2):
        for way in range(2):
            par(z, 0, way, c).start()

    last = ((0, 1), (2,)), ((0,), (1,))

    def step(t, final, between):
        zs = ((z + 16 - t) % 16, (z + t) % 16)
        for c in range(3):
            for way in range(2):
                own(zs[way], t - 1, way, c).wait_recv()
                if c in last[0][way]:
                    own(zs[way], t, way, c).start()
                elif final is None:
                    own(zs[way], t, way, c).start()
                else:
                    @pl.when(final)
                    def _():
                        own(zs[way], t, way, c).start()
                if c < 2:
                    side_send(zs[way], 2 * t - 1 + way, c).start()
            between(c)
        for c in range(2):
            for way in range(2):
                par(zs[way], t - 1, way, c).wait_recv()
                if c in last[1][way]:
                    par(zs[way], t, way, c).start()
                elif final is None:
                    par(zs[way], t, way, c).start()
                else:
                    @pl.when(final)
                    def _():
                        par(zs[way], t, way, c).start()
            between(3 + c)

    def b_events(t):
        def one(e):
            if (t, e) == (1, 2):
                for c in range(2):
                    remote(b_relay(c), b_relay(c), sb.at[0], rr.at[c], cross_x).wait_recv()
                    b_start(b_relay(c), b_slot(far_i, c), rb.at[far_i, c], side)
            if (t, e) == (1, 4):
                for d, c_on, peer in ((3, 0, yup), (1, 1, ydown)):
                    i = y_of(src, d)
                    for c in range(2):
                        b_wait(i, c)
                        if c == c_on:
                            b_pass(i, c, peer)
                        b_pass(i, c, twin)
            if (t, e) == (2, 2):
                for c in range(2):
                    b_wait(far_i, c)
                    b_pass(far_i, c, yup)
                    b_pass(far_i, c, ydown)
                    b_pass(far_i, c, twin)
            if (t, e) == (2, 4):
                for c in range(2):
                    b_wait(y_of(src, 2), c)
                    b_pass(y_of(src, 2), c, twin)
            if (t, e) == (3, 4):
                for d, c_on, peer in ((3, 0, yup), (1, 1, ydown)):
                    i = y_of(far_i, d)
                    for c in range(2):
                        b_wait(i, c)
                        if c == c_on:
                            b_pass(i, c, peer)
                        b_pass(i, c, twin)
            if (t, e) == (4, 2):
                for c in range(2):
                    b_wait(y_of(far_i, 2), c)
                    b_pass(y_of(far_i, 2), c, twin)
            if (t, e) == (4, 4):
                for base in (twin_i, (twin_i + 8) % 16):
                    for d in range(4):
                        for c in range(2):
                            b_wait((base // 8) * 8 + ((y + d) % 4) * 2 + 1 - low, c)

        return one

    for t in range(1, 5):
        step(t, None, b_events(t))
    for copy in local:
        copy.wait()
    for c in range(2):
        slot = units(z, col, SIDE[c])
        remote(slot, slot, sx.at[0, c], rx.at[0, c], side).wait_recv()

    def products(k, lo, hi_):
        zu, zd = (z + 16 - k) % 16, (z + k + 1) % 16

        def body(fp, carry):
            keep = (lanes // 32 == fp % 4).astype(F32).astype(BF16)
            for h in range(2):
                f = fp + 16 * h
                lhs = jnp.concatenate(
                    [
                        jnp.concatenate(
                            [a_all[pl.ds(zz * 2, 2), u, 8 * h : 8 * h + 16, :].reshape(32, 128) for zz in (zu, zd)],
                            axis=0,
                        )
                        for u in (fp, 16 + fp, 32 + fp // 4)
                    ],
                    axis=1,
                )
                rest = b_all[pl.ds(128 + 2 * (h * 4 + fp // 4), 2)].reshape(256, 128) * keep
                rhs = jnp.concatenate(
                    [
                        b_all[pl.ds(2 * f, 2)].reshape(256, 128),
                        b_all[pl.ds(64 + 2 * f, 2)].reshape(256, 128),
                        rest,
                    ],
                    axis=1,
                )
                r = lax.dot_general(lhs, rhs, NT, preferred_element_type=F32)
                pr = r[:, :128].reshape(8, 8, 128)
                qr = r[:, 128:].reshape(8, 8, 128)
                u = pr * wt[None] + pltpu.roll(qr, 4, 1) * wq
                u_ref[pl.ds(pl.multiple_of(f * 64, 64), 64), :] = u.reshape(64, 128)
            return carry

        lax.fori_loop(lo, hi_, body, 0)

    sel = l_ref[...]
    left = lax.broadcasted_iota(jnp.int32, (32, 128), 1) < 64

    def emit(k):
        zu, zd = (z + 16 - k) % 16, (z + k + 1) % 16

        def body(i4, carry):
            for part, zz in ((0, zu), (1, zd)):
                base = part * 32 + (i4 // 2) * 16 + i4 % 2
                rows = []
                for a in range(3):
                    for e in range(2):
                        r0 = (0, 2, 8)[a] + e * 4
                        r1 = (8, 10, 2)[a] + e * 4
                        rows.append(u_ref[pl.ds(base + r0, 16, stride=64), :])
                        rows.append(u_ref[pl.ds(16 * 64 + base + r1, 16, stride=64), :])
                xa = [jnp.concatenate(rows[4 * a : 4 * a + 4], axis=0).astype(BF16) for a in range(3)]
                rhs = jnp.concatenate([xa[0], xa[1], xa[1], xa[0], xa[2], xa[2]], axis=0)
                r = lax.dot_general(sel, rhs, NT, preferred_element_type=F32)
                t1, t2, t3 = r[:, :128], r[:, 128:256], r[:, 256:]
                b = lambda m, n: m[32 * n : 32 * n + 32]
                tiles = [
                    jnp.where(left, b(t1, 0), b(t2, 1)),
                    jnp.where(left, b(t1, 2), b(t1, 0)),
                    jnp.where(left, b(t2, 1), b(t1, 2)),
                    jnp.where(left, b(t3, 0), b(t3, 1)),
                    b(t3, 2)[:, :64],
                ]
                out_ref[zz * 4 + i4] = jnp.concatenate(tiles, axis=1).astype(BF16).reshape(16, 2, 576)
            return carry

        lax.fori_loop(0, 4, body, 0)

    def busy(t, carry):
        m = t - 5

        def between(e):
            if e == 0:
                for k in (1, 2):
                    side_recv(4 * m + k)
                products(2 * m, 0, 8)
            if e == 1:
                products(2 * m, 8, 16)
            if e == 2:
                emit(2 * m)
                for k in (3, 4):
                    side_recv(4 * m + k)
            if e == 3:
                products(2 * m + 1, 0, 8)
            if e == 4:
                products(2 * m + 1, 8, 16)
                emit(2 * m + 1)

        step(t, t < 7, between)
        return carry

    lax.fori_loop(5, 8, busy, 0)
    side_recv(13)
    side_recv(14)
    z8 = (z + 8) % 16

    def ending(k, carry):
        @pl.when(k == 7)
        def _():
            for c in range(3):
                way = 0 if c in last[0][0] else 1
                own(z8, 7, way, c).wait_recv()
                if c < 2:
                    side_send(z8, 15, c).start()
            for c in range(2):
                par(z8, 7, 0 if c in last[1][0] else 1, c).wait_recv()
            side_recv(15)

        products(k, 0, 16)
        emit(k)
        return carry

    lax.fori_loop(6, 8, ending, 0)

    def sent(t, carry):
        for way in range(2):
            for c in range(3):
                own(z, t, way, c).wait_send()
            for c in range(2):
                par(z, t, way, c).wait_send()
        return carry

    lax.fori_loop(0, 7, sent, 0)
    for way in range(2):
        for c in last[0][way]:
            own(z, 7, way, c).wait_send()
        for c in last[1][way]:
            par(z, 7, way, c).wait_send()
    for copy in side_first:
        copy.wait_send()

    def side_sent(k, carry):
        for c in range(2):
            side_send(z, k, c).wait_send()
        return carry

    lax.fori_loop(1, 16, side_sent, 0)
    for copy in b_sent:
        copy.wait_send()


def on_device(spectra, block_mask):
    count, segs, _ = spectra.shape
    ga, gb = jnp.asarray(source_selector(), BF16), jnp.asarray(receiver_selector(), BF16)
    vmem = pl.BlockSpec(memory_space=pltpu.VMEM)
    anyspace = pl.BlockSpec(memory_space=pl.ANY)
    dma = pltpu.SemaphoreType.DMA
    qa, qb = pl.pallas_call(
        arrange,
        out_shape=(jax.ShapeDtypeStruct((36, 24, 128), BF16), jax.ShapeDtypeStruct((144, 8, 128), BF16)),
        in_specs=[vmem] * 3,
        out_specs=[vmem] * 2,
        name="arrange",
    )(jnp.transpose(spectra, (1, 0, 2)), ga, gb)
    return pl.pallas_call(
        functools.partial(fused, 1.0 / math.sqrt(segs)),
        out_shape=jax.ShapeDtypeStruct((64, 16, 2, 576), BF16),
        in_specs=[anyspace, anyspace, vmem, vmem],
        out_specs=vmem,
        scratch_shapes=[
            pltpu.VMEM((32, 36, 24, 128), BF16),
            pltpu.VMEM((144, 128, 128), BF16),
            pltpu.VMEM((144, 8, 128), BF16),
            pltpu.VMEM((32 * 64, 128), F32),
            dma((2, 8, 3)), dma((2, 8, 3)), dma((2, 8, 2)), dma((2, 8, 2)),
            dma((17, 2)), dma((17, 2)), dma((48,)), dma((16, 2)), dma((2,)), dma((2,)),
        ],
        compiler_params=pltpu.CompilerParams(
            collective_id=0, has_side_effects=True, vmem_limit_bytes=56 * 1024 * 1024
        ),
        name="fused",
    )(qa, qb, block_mask, jnp.asarray(output_selector(), BF16))


def solution(mesh):
    return jax.shard_map(
        on_device,
        mesh=mesh,
        in_specs=(P(("src", "rcv"), None, None), P()),
        out_specs=P("src", None, "rcv", None),
        check_vma=False,
    )
```

```python
import functools
import math

import jax
import jax.numpy as jnp
import numpy as np
from jax import lax
from jax.experimental import pallas as pl
from jax.experimental.pallas import tpu as pltpu
from jax.sharding import PartitionSpec as P

MESH = pl.DeviceIdType.MESH
F32 = jnp.float32
BF16 = jnp.bfloat16
NT = (((1,), (1,)), ((), ()))


def source_selector():
    table = np.zeros((16, 24, 2, 192), np.float32)
    for fp in range(16):
        for c in range(2):
            for h in range(2):
                for s in range(2):
                    row = c * 4 + h * 2 + s
                    table[fp, row, s, h * 64 + c * 32 + fp] = 1
                    table[fp, 8 + row, s, 2 * 64 + c * 32 + fp + 16 * h] = 1
                    table[fp, 16 + row, s, h * 64 + c * 32 + fp + 16] = 1
    return table.reshape(384, 384)


def receiver_selector():
    table = np.zeros((32, 2, 4, 2, 2, 192), np.float32)
    for f in range(32):
        for c in range(2):
            for b in range(3):
                for s in range(2):
                    table[f, c, b, s, s, b * 64 + c * 32 + f] = 1
    return table.reshape(512, 384)


def output_selector():
    table = np.zeros((3, 16, 2, 16, 4, 2), np.float32)
    for b in range(3):
        for k in range(16):
            for s in range(2):
                table[b, k, s, k, b, s] = 1
    return table.reshape(96, 128)


def arrange(x_ref, ga_ref, gb_ref, qa_ref, qb_ref):
    segs = x_ref.shape[0]
    values = x_ref[...].astype(F32)
    mean_power = jnp.mean(values * values, axis=2, keepdims=True)
    white = (values * lax.rsqrt(mean_power + 1e-06))
    w = jnp.concatenate([white[:, 0, :], white[:, 1, :]], axis=1)
    w = jnp.concatenate([w, jnp.zeros((288 - segs, 384), F32)], axis=0).astype(BF16)
    ga, gb = ga_ref[...], gb_ref[...]
    ya = lax.dot_general(ga, w, NT, preferred_element_type=F32).astype(BF16)
    yb = lax.dot_general(gb, w, NT, preferred_element_type=F32).astype(BF16)
    for kt in range(2):
        qa_ref[kt * 16 : kt * 16 + 16] = ya[:, kt * 128 : kt * 128 + 128].reshape(16, 24, 128)
        qb_ref[kt * 64 : kt * 64 + 64] = yb[:, kt * 128 : kt * 128 + 128].reshape(64, 8, 128)
    rest = w[256:288]
    ga4 = ga.reshape(4, 4, 24, 384)
    gb4 = gb.reshape(8, 4, 16, 384)
    ta = jnp.zeros((96, 128), F32)
    tb = jnp.zeros((128, 128), F32)
    for q in range(4):
        parts = [rest if p == q else jnp.zeros_like(rest) for p in range(4)]
        placed = jnp.concatenate(parts, axis=0)
        ta += lax.dot_general(ga4[:, q].reshape(96, 384), placed, NT, preferred_element_type=F32)
        tb += lax.dot_general(gb4[:, q].reshape(128, 384), placed, NT, preferred_element_type=F32)
    qa_ref[32:36] = ta.astype(BF16).reshape(4, 24, 128)
    qb_ref[128:144] = tb.astype(BF16).reshape(16, 8, 128)


OWN = ((0, 10), (10, 20), (20, 36))
PAR = ((20, 28), (28, 36))
SIDE = OWN[:2]
HALVES = ((0, 72), (72, 144))
UNROLL = 4


def fused(scale, qa, qb, mask_ref, l_ref, out_ref, a_all, b_all, relay, u_ref,
          so, ro, sp, rp, sx, rx, sb, rb, rr, loc):
    src, rcv = lax.axis_index("src"), lax.axis_index("rcv")
    z, p = rcv // 2, rcv % 2
    col = 1 - p
    y = (src // 2) % 4
    hi, low = src // 8, src % 2
    far_i = (src + 8) % 16
    twin_i = src - low + (1 - low)
    up = (src, ((z + 1) % 16) * 2 + p)
    down = (src, ((z + 15) % 16) * 2 + p)
    side = (src, z * 2 + col)
    cross_x = (far_i, z * 2 + col)
    twin = (twin_i, rcv)

    def y_of(base, d):
        return (base // 8) * 8 + ((y + d) % 4) * 2 + low

    yup, ydown = (y_of(src, 1), rcv), (y_of(src, 3), rcv)
    peers = [up, down, side, cross_x, twin, yup, ydown]

    barrier = pltpu.get_barrier_semaphore()
    for peer in peers:
        pl.semaphore_signal(barrier, inc=1, device_id=peer, device_id_type=MESH)
    pl.semaphore_wait(barrier, len(peers))

    def remote(source, target, send, recv, peer):
        return pltpu.make_async_remote_copy(
            src_ref=source, dst_ref=target, send_sem=send, recv_sem=recv, device_id=peer, device_id_type=MESH
        )

    ways = ((0, up), (1, down))

    def units(zz, pp, span):
        return a_all.at[zz * 2 + pp, pl.ds(span[0], span[1] - span[0])]

    def own(zz, t, way, c, source=None):
        slot = units(zz, p, OWN[c])
        return remote(slot if source is None else source, slot, so.at[way, t, c], ro.at[way, t, c], ways[way][1])

    def par(zz, t, way, c):
        slot = units(zz, col, PAR[c])
        return remote(slot, slot, sp.at[way, t, c], rp.at[way, t, c], ways[way][1])

    def side_send(zz, k, c):
        slot = units(zz, p, SIDE[c])
        return remote(slot, slot, sx.at[k, c], rx.at[k, c], side)

    def side_recv(k):
        t = (k + 1) // 2
        zz = (z + (16 - t) * (k % 2) + t * (1 - k % 2)) % 16
        for c in range(2):
            slot = units(zz, col, SIDE[c])
            remote(slot, slot, sx.at[k, c], rx.at[k, c], side).wait_recv()

    b_sent = []

    def b_slot(i, c):
        lo, hi_ = HALVES[c]
        return b_all.at[pl.ds(lo, hi_ - lo), pl.ds(pl.multiple_of(i * 8, 8), 8)]

    def b_own(c):
        return qb.at[pl.ds(HALVES[c][0], HALVES[c][1] - HALVES[c][0])]

    def b_relay(c):
        return relay.at[pl.ds(HALVES[c][0], HALVES[c][1] - HALVES[c][0])]

    def b_start(source, target, recv, peer):
        copy = remote(source, target, sb.at[len(b_sent)], recv, peer)
        copy.start()
        b_sent.append(copy)

    def b_pass(i, c, peer):
        b_start(b_slot(i, c), b_slot(i, c), rb.at[i, c], peer)

    def b_wait(i, c):
        remote(b_slot(i, c), b_slot(i, c), sb.at[0], rb.at[i, c], twin).wait_recv()

    for c in range(2):
        b_start(b_own(c), b_relay(c), rr.at[c], cross_x)
        b_start(b_own(c), b_slot(src, c), rb.at[src, c], yup)
        b_start(b_own(c), b_slot(src, c), rb.at[src, c], ydown)
    for c in range(3):
        span = pl.ds(OWN[c][0], OWN[c][1] - OWN[c][0])
        for way in range(2):
            own(z, 0, way, c, qa.at[span]).start()
    side_first = []
    for c in (2, 0, 1):
        span = pl.ds(OWN[c][0], OWN[c][1] - OWN[c][0])
        slot = units(z, p, OWN[c])
        sem = (0, c) if c < 2 else (16, 0)
        side_first.append(remote(qa.at[span], slot, sx.at[sem], rx.at[sem], side))
    for copy in side_first:
        copy.start()
    for c in range(2):
        b_start(b_own(c), b_slot(src, c), rb.at[src, c], twin)
    local = [
        pltpu.make_async_copy(qa, a_all.at[z * 2 + p], loc.at[0]),
        pltpu.make_async_copy(qb, b_all.at[:, pl.ds(pl.multiple_of(src * 8, 8), 8)], loc.at[1]),
    ]
    for copy in local:
        copy.start()

    row = mask_ref[pl.ds(src, 1), :].astype(F32).astype(BF16)
    spread = lax.broadcasted_iota(jnp.int32, (16, 128), 1) // 8 == lax.broadcasted_iota(jnp.int32, (16, 128), 0)
    lanes = lax.broadcasted_iota(jnp.int32, (1, 128), 1)
    wt = jnp.dot(row, spread.astype(F32).astype(BF16), preferred_element_type=F32)
    wt = wt * jnp.where(lanes % 8 < 6, scale, 0.0)
    sign = jnp.where(lax.broadcasted_iota(jnp.int32, (8, 128), 0) < 4, 1.0, -1.0)
    wq = (wt * sign)[None]

    slot = units(z, col, OWN[2])
    remote(slot, slot, sx.at[16, 0], rx.at[16, 0], side).wait_recv()
    for c in range(2):
        for way in range(2):
            par(z, 0, way, c).start()

    last = ((0, 1), (2,)), ((0,), (1,))

    def step(t, final, between):
        zs = ((z + 16 - t) % 16, (z + t) % 16)
        for c in range(3):
            for way in range(2):
                own(zs[way], t - 1, way, c).wait_recv()
                if c in last[0][way]:
                    own(zs[way], t, way, c).start()
                elif final is None:
                    own(zs[way], t, way, c).start()
                else:
                    @pl.when(final)
                    def _():
                        own(zs[way], t, way, c).start()
                if c < 2:
                    side_send(zs[way], 2 * t - 1 + way, c).start()
            between(c)
        for c in range(2):
            for way in range(2):
                par(zs[way], t - 1, way, c).wait_recv()
                if c in last[1][way]:
                    par(zs[way], t, way, c).start()
                elif final is None:
                    par(zs[way], t, way, c).start()
                else:
                    @pl.when(final)
                    def _():
                        par(zs[way], t, way, c).start()
            between(3 + c)

    def b_events(t):
        def one(e):
            if (t, e) == (1, 2):
                for c in range(2):
                    remote(b_relay(c), b_relay(c), sb.at[0], rr.at[c], cross_x).wait_recv()
                    b_start(b_relay(c), b_slot(far_i, c), rb.at[far_i, c], side)
            if (t, e) == (1, 4):
                for d, c_on, peer in ((3, 0, yup), (1, 1, ydown)):
                    i = y_of(src, d)
                    for c in range(2):
                        b_wait(i, c)
                        if c == c_on:
                            b_pass(i, c, peer)
                        b_pass(i, c, twin)
            if (t, e) == (2, 2):
                for c in range(2):
                    b_wait(far_i, c)
                    b_pass(far_i, c, yup)
                    b_pass(far_i, c, ydown)
                    b_pass(far_i, c, twin)
            if (t, e) == (2, 4):
                for c in range(2):
                    b_wait(y_of(src, 2), c)
                    b_pass(y_of(src, 2), c, twin)
            if (t, e) == (3, 4):
                for d, c_on, peer in ((3, 0, yup), (1, 1, ydown)):
                    i = y_of(far_i, d)
                    for c in range(2):
                        b_wait(i, c)
                        if c == c_on:
                            b_pass(i, c, peer)
                        b_pass(i, c, twin)
            if (t, e) == (4, 2):
                for c in range(2):
                    b_wait(y_of(far_i, 2), c)
                    b_pass(y_of(far_i, 2), c, twin)
            if (t, e) == (4, 4):
                for base in (twin_i, (twin_i + 8) % 16):
                    for d in range(4):
                        for c in range(2):
                            b_wait((base // 8) * 8 + ((y + d) % 4) * 2 + 1 - low, c)

        return one

    for t in range(1, 5):
        step(t, None, b_events(t))
    for copy in local:
        copy.wait()
    for c in range(2):
        slot = units(z, col, SIDE[c])
        remote(slot, slot, sx.at[0, c], rx.at[0, c], side).wait_recv()

    def products(zs, lo, hi_):
        rows = 32 * len(zs)

        def body(fp, carry):
            keep = (lanes // 32 == fp % 4).astype(F32).astype(BF16)
            for h in range(2):
                f = fp + 16 * h
                lhs = jnp.concatenate(
                    [
                        jnp.concatenate(
                            [a_all[pl.ds(zz * 2, 2), u, 8 * h : 8 * h + 16, :].reshape(32, 128) for zz in zs], axis=0
                        )
                        for u in (fp, 16 + fp, 32 + fp // 4)
                    ],
                    axis=1,
                )
                rest = b_all[pl.ds(128 + 2 * (h * 4 + fp // 4), 2)].reshape(256, 128) * keep
                rhs = jnp.concatenate(
                    [
                        b_all[pl.ds(2 * f, 2)].reshape(256, 128),
                        b_all[pl.ds(64 + 2 * f, 2)].reshape(256, 128),
                        rest,
                    ],
                    axis=1,
                )
                r = lax.dot_general(lhs, rhs, NT, preferred_element_type=F32)
                pr = r[:, :128].reshape(rows // 8, 8, 128)
                qr = r[:, 128:].reshape(rows // 8, 8, 128)
                u = pr * wt[None] + pltpu.roll(qr, 4, 1) * wq
                u_ref[pl.ds(pl.multiple_of(f * 128, 128), rows), :] = u.reshape(rows, 128)
            return carry

        lax.fori_loop(lo, hi_, body, 0, unroll=UNROLL)

    sel = l_ref[...]
    left = lax.broadcasted_iota(jnp.int32, (32, 128), 1) < 64

    def emit(zs, lo, hi_):
        def body(i4, carry):
            for part, zz in enumerate(zs):
                base = part * 32 + (i4 // 2) * 16 + i4 % 2
                rows = []
                for a in range(3):
                    for e in range(2):
                        r0 = (0, 2, 8)[a] + e * 4
                        r1 = (8, 10, 2)[a] + e * 4
                        rows.append(u_ref[pl.ds(base + r0, 16, stride=128), :])
                        rows.append(u_ref[pl.ds(16 * 128 + base + r1, 16, stride=128), :])
                xa = [jnp.concatenate(rows[4 * a : 4 * a + 4], axis=0).astype(BF16) for a in range(3)]
                rhs = jnp.concatenate([xa[0], xa[1], xa[1], xa[0], xa[2], xa[2]], axis=0)
                r = lax.dot_general(sel, rhs, NT, preferred_element_type=F32)
                t1, t2, t3 = r[:, :128], r[:, 128:256], r[:, 256:]
                b = lambda m, n: m[32 * n : 32 * n + 32]
                tiles = [
                    jnp.where(left, b(t1, 0), b(t2, 1)),
                    jnp.where(left, b(t1, 2), b(t1, 0)),
                    jnp.where(left, b(t2, 1), b(t1, 2)),
                    jnp.where(left, b(t3, 0), b(t3, 1)),
                    b(t3, 2)[:, :64],
                ]
                out_ref[zz * 4 + i4] = jnp.concatenate(tiles, axis=1).astype(BF16).reshape(16, 2, 576)
            return carry

        lax.fori_loop(lo, hi_, body, 0)

    def busy(t, carry):
        m = t - 5
        zs = [(z + 16 - 2 * m) % 16, (z + 2 * m + 1) % 16, (z + 15 - 2 * m) % 16, (z + 2 * m + 2) % 16]

        def between(e):
            if e == 0:
                for k in range(1, 5):
                    side_recv(4 * m + k)
                products(zs, 0, 4)
            if e == 1:
                products(zs, 4, 8)
            if e == 2:
                products(zs, 8, 16)
            if e == 3:
                emit(zs, 0, 2)
            if e == 4:
                emit(zs, 2, 4)

        step(t, t < 7, between)
        return carry

    lax.fori_loop(5, 8, busy, 0)
    side_recv(13)
    side_recv(14)
    z8 = (z + 8) % 16

    def ending(k, carry):
        @pl.when(k == 7)
        def _():
            for c in range(3):
                way = 0 if c in last[0][0] else 1
                own(z8, 7, way, c).wait_recv()
                if c < 2:
                    side_send(z8, 15, c).start()
            for c in range(2):
                par(z8, 7, 0 if c in last[1][0] else 1, c).wait_recv()
            side_recv(15)

        zs = [(z + 16 - k) % 16, (z + k + 1) % 16]
        products(zs, 0, 16)
        emit(zs, 0, 4)
        return carry

    lax.fori_loop(6, 8, ending, 0)

    def sent(t, carry):
        for way in range(2):
            for c in range(3):
                own(z, t, way, c).wait_send()
            for c in range(2):
                par(z, t, way, c).wait_send()
        return carry

    lax.fori_loop(0, 7, sent, 0)
    for way in range(2):
        for c in last[0][way]:
            own(z, 7, way, c).wait_send()
        for c in last[1][way]:
            par(z, 7, way, c).wait_send()
    for copy in side_first:
        copy.wait_send()

    def side_sent(k, carry):
        for c in range(2):
            side_send(z, k, c).wait_send()
        return carry

    lax.fori_loop(1, 16, side_sent, 0)
    for copy in b_sent:
        copy.wait_send()


def hand_over(x_ref, out_ref):
    out_ref[...] = x_ref[...]


def on_device(spectra, block_mask):
    count, segs, _ = spectra.shape
    ga, gb = jnp.asarray(source_selector(), BF16), jnp.asarray(receiver_selector(), BF16)
    vmem = pl.BlockSpec(memory_space=pltpu.VMEM)
    anyspace = pl.BlockSpec(memory_space=pl.ANY)
    dma = pltpu.SemaphoreType.DMA
    qa, qb = pl.pallas_call(
        arrange,
        out_shape=(jax.ShapeDtypeStruct((36, 24, 128), BF16), jax.ShapeDtypeStruct((144, 8, 128), BF16)),
        in_specs=[vmem] * 3,
        out_specs=[vmem] * 2,
        name="arrange",
    )(jnp.transpose(spectra, (1, 0, 2)), ga, gb)
    out = pl.pallas_call(
        functools.partial(fused, 1.0 / math.sqrt(segs)),
        out_shape=jax.ShapeDtypeStruct((64, 16, 2, 576), BF16),
        in_specs=[anyspace, anyspace, vmem, vmem],
        out_specs=vmem,
        scratch_shapes=[
            pltpu.VMEM((32, 36, 24, 128), BF16),
            pltpu.VMEM((144, 128, 128), BF16),
            pltpu.VMEM((144, 8, 128), BF16),
            pltpu.VMEM((32 * 128, 128), F32),
            dma((2, 8, 3)), dma((2, 8, 3)), dma((2, 8, 2)), dma((2, 8, 2)),
            dma((17, 2)), dma((17, 2)), dma((48,)), dma((16, 2)), dma((2,)), dma((2,)),
        ],
        compiler_params=pltpu.CompilerParams(
            collective_id=0, has_side_effects=True, vmem_limit_bytes=56 * 1024 * 1024
        ),
        name="fused",
    )(qa, qb, block_mask, jnp.asarray(output_selector(), BF16))
    block = pl.BlockSpec((64 // 2, 16, 2, 576), lambda i: (i, 0, 0, 0))
    return pl.pallas_call(
        hand_over,
        grid=(2,),
        out_shape=jax.ShapeDtypeStruct((64, 16, 2, 576), BF16),
        in_specs=[block],
        out_specs=block,
        name="hand_over",
    )(out)


def solution(mesh):
    return jax.shard_map(
        on_device,
        mesh=mesh,
        in_specs=(P(("src", "rcv"), None, None), P()),
        out_specs=P("src", None, "rcv", None),
        check_vma=False,
    )
```

```python
import functools
import math

import jax
import jax.numpy as jnp
import numpy as np
from jax import lax
from jax.experimental import pallas as pl
from jax.experimental.pallas import tpu as pltpu
from jax.sharding import PartitionSpec as P

MESH = pl.DeviceIdType.MESH
F32 = jnp.float32
BF16 = jnp.bfloat16
NT = (((1,), (1,)), ((), ()))


def source_selector():
    table = np.zeros((16, 24, 2, 192), np.float32)
    for fp in range(16):
        for c in range(2):
            for h in range(2):
                for s in range(2):
                    row = c * 4 + h * 2 + s
                    table[fp, row, s, h * 64 + c * 32 + fp] = 1
                    table[fp, 8 + row, s, 2 * 64 + c * 32 + fp + 16 * h] = 1
                    table[fp, 16 + row, s, h * 64 + c * 32 + fp + 16] = 1
    return table.reshape(384, 384)


def receiver_selector():
    table = np.zeros((32, 2, 4, 2, 2, 192), np.float32)
    for f in range(32):
        for c in range(2):
            for b in range(3):
                for s in range(2):
                    table[f, c, b, s, s, b * 64 + c * 32 + f] = 1
    return table.reshape(512, 384)


def output_selector():
    table = np.zeros((3, 16, 2, 16, 4, 2), np.float32)
    for b in range(3):
        for k in range(16):
            for s in range(2):
                table[b, k, s, k, b, s] = 1
    return table.reshape(96, 128)


def whitened(x_ref):
    segs = x_ref.shape[0]
    values = x_ref[...].astype(F32)
    mean_power = jnp.mean(values * values, axis=2, keepdims=True)
    white = values * lax.rsqrt(mean_power + 1e-06)
    w = jnp.concatenate([white[:, 0, :], white[:, 1, :]], axis=1)
    return jnp.concatenate([w, jnp.zeros((288 - segs, 384), F32)], axis=0).astype(BF16)


def arrange(w, selector, out_ref, groups, rows):
    whole = lax.dot_general(selector, w, NT, preferred_element_type=F32).astype(BF16)
    unit = out_ref.shape[1]
    count = selector.shape[0] // unit
    for kt in range(2):
        out_ref[kt * count : kt * count + count] = whole[:, kt * 128 : kt * 128 + 128].reshape(count, unit, 128)
    rest = w[256:288]
    parts = selector.reshape(groups, 4, rows, 384)
    total = jnp.zeros((groups * rows, 128), F32)
    for q in range(4):
        placed = jnp.concatenate([rest if n == q else jnp.zeros_like(rest) for n in range(4)], axis=0)
        chosen = parts[:, q].reshape(groups * rows, 384)
        total += lax.dot_general(chosen, placed, NT, preferred_element_type=F32)
    tail = groups * rows // unit
    out_ref[2 * count : 2 * count + tail] = total.astype(BF16).reshape(tail, unit, 128)


OWN = ((0, 10), (10, 20), (20, 36))
PAR = ((20, 28), (28, 36))
SIDE = OWN[:2]
HALVES = ((0, 72), (72, 144))
UNROLL = 4


def fused(scale, x_ref, ga_ref, gb_ref, mask_ref, l_ref, out_ref, qa, qb, a_all, b_all, relay, u_ref,
          so, ro, sp, rp, sx, rx, sb, rb, rr, loc):
    src, rcv = lax.axis_index("src"), lax.axis_index("rcv")
    z, p = rcv // 2, rcv % 2
    col = 1 - p
    y = (src // 2) % 4
    hi, low = src // 8, src % 2
    far_i = (src + 8) % 16
    twin_i = src - low + (1 - low)
    up = (src, ((z + 1) % 16) * 2 + p)
    down = (src, ((z + 15) % 16) * 2 + p)
    side = (src, z * 2 + col)
    cross_x = (far_i, z * 2 + col)
    twin = (twin_i, rcv)

    def y_of(base, d):
        return (base // 8) * 8 + ((y + d) % 4) * 2 + low

    yup, ydown = (y_of(src, 1), rcv), (y_of(src, 3), rcv)
    peers = [up, down, side, cross_x, twin, yup, ydown]

    barrier = pltpu.get_barrier_semaphore()
    for peer in peers:
        pl.semaphore_signal(barrier, inc=1, device_id=peer, device_id_type=MESH)
    w = whitened(x_ref)
    arrange(w, ga_ref[...], qa, 4, 24)
    pl.semaphore_wait(barrier, len(peers))

    def remote(source, target, send, recv, peer):
        return pltpu.make_async_remote_copy(
            src_ref=source, dst_ref=target, send_sem=send, recv_sem=recv, device_id=peer, device_id_type=MESH
        )

    ways = ((0, up), (1, down))

    def units(zz, pp, span):
        return a_all.at[zz * 2 + pp, pl.ds(span[0], span[1] - span[0])]

    def own(zz, t, way, c, source=None):
        slot = units(zz, p, OWN[c])
        return remote(slot if source is None else source, slot, so.at[way, t, c], ro.at[way, t, c], ways[way][1])

    def par(zz, t, way, c):
        slot = units(zz, col, PAR[c])
        return remote(slot, slot, sp.at[way, t, c], rp.at[way, t, c], ways[way][1])

    def side_send(zz, k, c):
        slot = units(zz, p, SIDE[c])
        return remote(slot, slot, sx.at[k, c], rx.at[k, c], side)

    def side_recv(k):
        t = (k + 1) // 2
        zz = (z + (16 - t) * (k % 2) + t * (1 - k % 2)) % 16
        for c in range(2):
            slot = units(zz, col, SIDE[c])
            remote(slot, slot, sx.at[k, c], rx.at[k, c], side).wait_recv()

    b_sent = []

    def b_slot(i, c):
        lo, hi_ = HALVES[c]
        return b_all.at[pl.ds(lo, hi_ - lo), pl.ds(pl.multiple_of(i * 8, 8), 8)]

    def b_own(c):
        return qb.at[pl.ds(HALVES[c][0], HALVES[c][1] - HALVES[c][0])]

    def b_relay(c):
        return relay.at[pl.ds(HALVES[c][0], HALVES[c][1] - HALVES[c][0])]

    def b_start(source, target, recv, peer):
        copy = remote(source, target, sb.at[len(b_sent)], recv, peer)
        copy.start()
        b_sent.append(copy)

    def b_pass(i, c, peer):
        b_start(b_slot(i, c), b_slot(i, c), rb.at[i, c], peer)

    def b_wait(i, c):
        remote(b_slot(i, c), b_slot(i, c), sb.at[0], rb.at[i, c], twin).wait_recv()

    for c in range(3):
        span = pl.ds(OWN[c][0], OWN[c][1] - OWN[c][0])
        for way in range(2):
            own(z, 0, way, c, qa.at[span]).start()
    side_first = []
    for c in (2, 0, 1):
        span = pl.ds(OWN[c][0], OWN[c][1] - OWN[c][0])
        slot = units(z, p, OWN[c])
        sem = (0, c) if c < 2 else (16, 0)
        side_first.append(remote(qa.at[span], slot, sx.at[sem], rx.at[sem], side))
    for copy in side_first:
        copy.start()
    arrange(w, gb_ref[...], qb, 8, 16)
    for c in range(2):
        b_start(b_own(c), b_relay(c), rr.at[c], cross_x)
        b_start(b_own(c), b_slot(src, c), rb.at[src, c], yup)
        b_start(b_own(c), b_slot(src, c), rb.at[src, c], ydown)
    for c in range(2):
        b_start(b_own(c), b_slot(src, c), rb.at[src, c], twin)
    local = [
        pltpu.make_async_copy(qa, a_all.at[z * 2 + p], loc.at[0]),
        pltpu.make_async_copy(qb, b_all.at[:, pl.ds(pl.multiple_of(src * 8, 8), 8)], loc.at[1]),
    ]
    for copy in local:
        copy.start()

    row = mask_ref[pl.ds(src, 1), :].astype(F32).astype(BF16)
    spread = lax.broadcasted_iota(jnp.int32, (16, 128), 1) // 8 == lax.broadcasted_iota(jnp.int32, (16, 128), 0)
    lanes = lax.broadcasted_iota(jnp.int32, (1, 128), 1)
    wt = jnp.dot(row, spread.astype(F32).astype(BF16), preferred_element_type=F32)
    wt = wt * jnp.where(lanes % 8 < 6, scale, 0.0)
    sign = jnp.where(lax.broadcasted_iota(jnp.int32, (8, 128), 0) < 4, 1.0, -1.0)
    wq = (wt * sign)[None]

    slot = units(z, col, OWN[2])
    remote(slot, slot, sx.at[16, 0], rx.at[16, 0], side).wait_recv()
    for c in range(2):
        for way in range(2):
            par(z, 0, way, c).start()

    last = ((0, 1), (2,)), ((0,), (1,))

    def step(t, final, between):
        zs = ((z + 16 - t) % 16, (z + t) % 16)
        for c in range(3):
            for way in range(2):
                own(zs[way], t - 1, way, c).wait_recv()
                if c in last[0][way]:
                    own(zs[way], t, way, c).start()
                elif final is None:
                    own(zs[way], t, way, c).start()
                else:
                    @pl.when(final)
                    def _():
                        own(zs[way], t, way, c).start()
                if c < 2:
                    side_send(zs[way], 2 * t - 1 + way, c).start()
            between(c)
        for c in range(2):
            for way in range(2):
                par(zs[way], t - 1, way, c).wait_recv()
                if c in last[1][way]:
                    par(zs[way], t, way, c).start()
                elif final is None:
                    par(zs[way], t, way, c).start()
                else:
                    @pl.when(final)
                    def _():
                        par(zs[way], t, way, c).start()
            between(3 + c)

    def b_events(t):
        def one(e):
            if (t, e) == (1, 2):
                for c in range(2):
                    remote(b_relay(c), b_relay(c), sb.at[0], rr.at[c], cross_x).wait_recv()
                    b_start(b_relay(c), b_slot(far_i, c), rb.at[far_i, c], side)
            if (t, e) == (1, 4):
                for d, c_on, peer in ((3, 0, yup), (1, 1, ydown)):
                    i = y_of(src, d)
                    for c in range(2):
                        b_wait(i, c)
                        if c == c_on:
                            b_pass(i, c, peer)
                        b_pass(i, c, twin)
            if (t, e) == (2, 2):
                for c in range(2):
                    b_wait(far_i, c)
                    b_pass(far_i, c, yup)
                    b_pass(far_i, c, ydown)
                    b_pass(far_i, c, twin)
            if (t, e) == (2, 4):
                for c in range(2):
                    b_wait(y_of(src, 2), c)
                    b_pass(y_of(src, 2), c, twin)
            if (t, e) == (3, 4):
                for d, c_on, peer in ((3, 0, yup), (1, 1, ydown)):
                    i = y_of(far_i, d)
                    for c in range(2):
                        b_wait(i, c)
                        if c == c_on:
                            b_pass(i, c, peer)
                        b_pass(i, c, twin)
            if (t, e) == (4, 2):
                for c in range(2):
                    b_wait(y_of(far_i, 2), c)
                    b_pass(y_of(far_i, 2), c, twin)
            if (t, e) == (4, 4):
                for base in (twin_i, (twin_i + 8) % 16):
                    for d in range(4):
                        for c in range(2):
                            b_wait((base // 8) * 8 + ((y + d) % 4) * 2 + 1 - low, c)

        return one

    for t in range(1, 5):
        step(t, None, b_events(t))
    for copy in local:
        copy.wait()
    for c in range(2):
        slot = units(z, col, SIDE[c])
        remote(slot, slot, sx.at[0, c], rx.at[0, c], side).wait_recv()

    def products(zs, lo, hi_):
        rows = 32 * len(zs)

        def body(fp, carry):
            keep = (lanes // 32 == fp % 4).astype(F32).astype(BF16)
            for h in range(2):
                f = fp + 16 * h
                lhs = jnp.concatenate(
                    [
                        jnp.concatenate(
                            [a_all[pl.ds(zz * 2, 2), u, 8 * h : 8 * h + 16, :].reshape(32, 128) for zz in zs], axis=0
                        )
                        for u in (fp, 16 + fp, 32 + fp // 4)
                    ],
                    axis=1,
                )
                rest = b_all[pl.ds(128 + 2 * (h * 4 + fp // 4), 2)].reshape(256, 128) * keep
                rhs = jnp.concatenate(
                    [
                        b_all[pl.ds(2 * f, 2)].reshape(256, 128),
                        b_all[pl.ds(64 + 2 * f, 2)].reshape(256, 128),
                        rest,
                    ],
                    axis=1,
                )
                r = lax.dot_general(lhs, rhs, NT, preferred_element_type=F32)
                pr = r[:, :128].reshape(rows // 8, 8, 128)
                qr = r[:, 128:].reshape(rows // 8, 8, 128)
                u = pr * wt[None] + pltpu.roll(qr, 4, 1) * wq
                u_ref[pl.ds(pl.multiple_of(f * 128, 128), rows), :] = u.reshape(rows, 128)
            return carry

        lax.fori_loop(lo, hi_, body, 0, unroll=UNROLL)

    sel = l_ref[...]
    left = lax.broadcasted_iota(jnp.int32, (32, 128), 1) < 64

    def emit(zs, lo, hi_, unroll=1):
        def body(i4, carry):
            for part, zz in enumerate(zs):
                base = part * 32 + (i4 // 2) * 16 + i4 % 2
                rows = []
                for a in range(3):
                    for e in range(2):
                        r0 = (0, 2, 8)[a] + e * 4
                        r1 = (8, 10, 2)[a] + e * 4
                        rows.append(u_ref[pl.ds(base + r0, 16, stride=128), :])
                        rows.append(u_ref[pl.ds(16 * 128 + base + r1, 16, stride=128), :])
                xa = [jnp.concatenate(rows[4 * a : 4 * a + 4], axis=0).astype(BF16) for a in range(3)]
                rhs = jnp.concatenate([xa[0], xa[1], xa[1], xa[0], xa[2], xa[2]], axis=0)
                r = lax.dot_general(sel, rhs, NT, preferred_element_type=F32)
                t1, t2, t3 = r[:, :128], r[:, 128:256], r[:, 256:]
                b = lambda m, n: m[32 * n : 32 * n + 32]
                tiles = [
                    jnp.where(left, b(t1, 0), b(t2, 1)),
                    jnp.where(left, b(t1, 2), b(t1, 0)),
                    jnp.where(left, b(t2, 1), b(t1, 2)),
                    jnp.where(left, b(t3, 0), b(t3, 1)),
                    b(t3, 2)[:, :64],
                ]
                out_ref[zz * 4 + i4] = jnp.concatenate(tiles, axis=1).astype(BF16).reshape(16, 2, 576)
            return carry

        lax.fori_loop(lo, hi_, body, 0, unroll=unroll)

    def busy(t, carry):
        m = t - 5
        zs = [(z + 16 - 2 * m) % 16, (z + 2 * m + 1) % 16, (z + 15 - 2 * m) % 16, (z + 2 * m + 2) % 16]

        def between(e):
            if e == 0:
                for k in range(1, 5):
                    side_recv(4 * m + k)
                products(zs, 0, 4)
            if e == 1:
                products(zs, 4, 8)
            if e == 2:
                products(zs, 8, 16)
            if e == 3:
                emit(zs, 0, 2)
            if e == 4:
                emit(zs, 2, 4)

        step(t, t < 7, between)
        return carry

    lax.fori_loop(5, 8, busy, 0)
    side_recv(13)
    side_recv(14)
    z8 = (z + 8) % 16

    zs = [(z + 10) % 16, (z + 7) % 16, (z + 9) % 16]
    products(zs, 0, 16)
    for c in range(3):
        way = 0 if c in last[0][0] else 1
        own(z8, 7, way, c).wait_recv()
        if c < 2:
            side_send(z8, 15, c).start()
    emit(zs, 0, 4)
    for c in range(2):
        par(z8, 7, 0 if c in last[1][0] else 1, c).wait_recv()
    side_recv(15)
    products([z8], 0, 16)
    emit([z8], 0, 4, 4)

    def sent(t, carry):
        for way in range(2):
            for c in range(3):
                own(z, t, way, c).wait_send()
            for c in range(2):
                par(z, t, way, c).wait_send()
        return carry

    lax.fori_loop(0, 7, sent, 0)
    for way in range(2):
        for c in last[0][way]:
            own(z, 7, way, c).wait_send()
        for c in last[1][way]:
            par(z, 7, way, c).wait_send()
    for copy in side_first:
        copy.wait_send()

    def side_sent(k, carry):
        for c in range(2):
            side_send(z, k, c).wait_send()
        return carry

    lax.fori_loop(1, 16, side_sent, 0)
    for copy in b_sent:
        copy.wait_send()


def hand_over(x_ref, out_ref):
    out_ref[...] = x_ref[...]


def on_device(spectra, block_mask):
    count, segs, _ = spectra.shape
    ga, gb = jnp.asarray(source_selector(), BF16), jnp.asarray(receiver_selector(), BF16)
    vmem = pl.BlockSpec(memory_space=pltpu.VMEM)
    dma = pltpu.SemaphoreType.DMA
    out = pl.pallas_call(
        functools.partial(fused, 1.0 / math.sqrt(segs)),
        out_shape=jax.ShapeDtypeStruct((64, 16, 2, 576), BF16),
        in_specs=[vmem] * 5,
        out_specs=vmem,
        scratch_shapes=[
            pltpu.VMEM((36, 24, 128), BF16),
            pltpu.VMEM((144, 8, 128), BF16),
            pltpu.VMEM((32, 36, 24, 128), BF16),
            pltpu.VMEM((144, 128, 128), BF16),
            pltpu.VMEM((144, 8, 128), BF16),
            pltpu.VMEM((32 * 128, 128), F32),
            dma((2, 8, 3)), dma((2, 8, 3)), dma((2, 8, 2)), dma((2, 8, 2)),
            dma((17, 2)), dma((17, 2)), dma((48,)), dma((16, 2)), dma((2,)), dma((2,)),
        ],
        compiler_params=pltpu.CompilerParams(
            collective_id=0, has_side_effects=True, vmem_limit_bytes=56 * 1024 * 1024
        ),
        name="fused",
    )(jnp.transpose(spectra, (1, 0, 2)), ga, gb, block_mask, jnp.asarray(output_selector(), BF16))
    block = pl.BlockSpec((64 // 2, 16, 2, 576), lambda i: (i, 0, 0, 0))
    return pl.pallas_call(
        hand_over,
        grid=(2,),
        out_shape=jax.ShapeDtypeStruct((64, 16, 2, 576), BF16),
        in_specs=[block],
        out_specs=block,
        name="hand_over",
    )(out)


def solution(mesh):
    return jax.shard_map(
        on_device,
        mesh=mesh,
        in_specs=(P(("src", "rcv"), None, None), P()),
        out_specs=P("src", None, "rcv", None),
        check_vma=False,
    )
```

```python
import functools
import math

import jax
import jax.numpy as jnp
import numpy as np
from jax import lax
from jax.experimental import pallas as pl
from jax.experimental.pallas import tpu as pltpu
from jax.sharding import PartitionSpec as P

MESH = pl.DeviceIdType.MESH
F32 = jnp.float32
BF16 = jnp.bfloat16
NT = (((1,), (1,)), ((), ()))


def source_selector():
    table = np.zeros((16, 24, 2, 192), np.float32)
    for fp in range(16):
        for c in range(2):
            for h in range(2):
                for s in range(2):
                    row = c * 4 + h * 2 + s
                    table[fp, row, s, h * 64 + c * 32 + fp] = 1
                    table[fp, 8 + row, s, 2 * 64 + c * 32 + fp + 16 * h] = 1
                    table[fp, 16 + row, s, h * 64 + c * 32 + fp + 16] = 1
    return table.reshape(384, 384)


def receiver_selector():
    table = np.zeros((32, 2, 4, 2, 2, 192), np.float32)
    for f in range(32):
        for c in range(2):
            for b in range(3):
                for s in range(2):
                    table[f, c, b, s, s, b * 64 + c * 32 + f] = 1
    return table.reshape(512, 384)


def output_selector():
    table = np.zeros((3, 16, 2, 16, 4, 2), np.float32)
    for b in range(3):
        for k in range(16):
            for s in range(2):
                table[b, k, s, k, b, s] = 1
    return table.reshape(96, 128)


def whitened(x_ref):
    segs = x_ref.shape[0]
    values = x_ref[...].astype(F32)
    mean_power = jnp.mean(values * values, axis=2, keepdims=True)
    white = values * lax.rsqrt(mean_power + 1e-06)
    w = jnp.concatenate([white[:, 0, :], white[:, 1, :]], axis=1)
    return jnp.concatenate([w, jnp.zeros((288 - segs, 384), F32)], axis=0).astype(BF16)


def arrange(w, selector, out_ref, groups, rows):
    whole = lax.dot_general(selector, w, NT, preferred_element_type=F32).astype(BF16)
    unit = out_ref.shape[1]
    count = selector.shape[0] // unit
    for kt in range(2):
        out_ref[kt * count : kt * count + count] = whole[:, kt * 128 : kt * 128 + 128].reshape(count, unit, 128)
    rest = w[256:288]
    parts = selector.reshape(groups, 4, rows, 384)
    total = jnp.zeros((groups * rows, 128), F32)
    for q in range(4):
        placed = jnp.concatenate([rest if n == q else jnp.zeros_like(rest) for n in range(4)], axis=0)
        chosen = parts[:, q].reshape(groups * rows, 384)
        total += lax.dot_general(chosen, placed, NT, preferred_element_type=F32)
    tail = groups * rows // unit
    out_ref[2 * count : 2 * count + tail] = total.astype(BF16).reshape(tail, unit, 128)


OWN = ((0, 10), (10, 20), (20, 36))
PAR = ((20, 28), (28, 36))
SIDE = OWN[:2]
HALVES = ((0, 72), (72, 144))
UNROLL = 4


def fused(scale, x_ref, table_ref, mask_ref, out_ref, qa, qb, a_all, b_all, relay, u_ref,
          so, ro, sp, rp, sx, rx, sb, rb, rr, loc):
    src, rcv = lax.axis_index("src"), lax.axis_index("rcv")
    z, p = rcv // 2, rcv % 2
    col = 1 - p
    y = (src // 2) % 4
    hi, low = src // 8, src % 2
    far_i = (src + 8) % 16
    twin_i = src - low + (1 - low)
    up = (src, ((z + 1) % 16) * 2 + p)
    down = (src, ((z + 15) % 16) * 2 + p)
    side = (src, z * 2 + col)
    cross_x = (far_i, z * 2 + col)
    twin = (twin_i, rcv)

    def y_of(base, d):
        return (base // 8) * 8 + ((y + d) % 4) * 2 + low

    yup, ydown = (y_of(src, 1), rcv), (y_of(src, 3), rcv)
    peers = [up, down, side, cross_x, twin, yup, ydown]

    barrier = pltpu.get_barrier_semaphore()
    for peer in peers:
        pl.semaphore_signal(barrier, inc=1, device_id=peer, device_id_type=MESH)
    w = whitened(x_ref)
    arrange(w, table_ref[0:384], qa, 4, 24)
    pl.semaphore_wait(barrier, len(peers))

    def remote(source, target, send, recv, peer):
        return pltpu.make_async_remote_copy(
            src_ref=source, dst_ref=target, send_sem=send, recv_sem=recv, device_id=peer, device_id_type=MESH
        )

    ways = ((0, up), (1, down))

    def units(zz, pp, span):
        return a_all.at[zz * 2 + pp, pl.ds(span[0], span[1] - span[0])]

    def own(zz, t, way, c, source=None):
        slot = units(zz, p, OWN[c])
        return remote(slot if source is None else source, slot, so.at[way, t, c], ro.at[way, t, c], ways[way][1])

    def par(zz, t, way, c):
        slot = units(zz, col, PAR[c])
        return remote(slot, slot, sp.at[way, t, c], rp.at[way, t, c], ways[way][1])

    def side_send(zz, k, c):
        slot = units(zz, p, SIDE[c])
        return remote(slot, slot, sx.at[k, c], rx.at[k, c], side)

    def side_recv(k):
        t = (k + 1) // 2
        zz = (z + (16 - t) * (k % 2) + t * (1 - k % 2)) % 16
        for c in range(2):
            slot = units(zz, col, SIDE[c])
            remote(slot, slot, sx.at[k, c], rx.at[k, c], side).wait_recv()

    b_sent = []

    def b_slot(i, c):
        lo, hi_ = HALVES[c]
        return b_all.at[pl.ds(lo, hi_ - lo), pl.ds(pl.multiple_of(i * 8, 8), 8)]

    def b_own(c):
        return qb.at[pl.ds(HALVES[c][0], HALVES[c][1] - HALVES[c][0])]

    def b_relay(c):
        return relay.at[pl.ds(HALVES[c][0], HALVES[c][1] - HALVES[c][0])]

    def b_start(source, target, recv, peer):
        copy = remote(source, target, sb.at[len(b_sent)], recv, peer)
        copy.start()
        b_sent.append(copy)

    def b_pass(i, c, peer):
        b_start(b_slot(i, c), b_slot(i, c), rb.at[i, c], peer)

    def b_wait(i, c):
        remote(b_slot(i, c), b_slot(i, c), sb.at[0], rb.at[i, c], twin).wait_recv()

    for c in range(3):
        span = pl.ds(OWN[c][0], OWN[c][1] - OWN[c][0])
        for way in range(2):
            own(z, 0, way, c, qa.at[span]).start()
    side_first = []
    for c in (2, 0, 1):
        span = pl.ds(OWN[c][0], OWN[c][1] - OWN[c][0])
        slot = units(z, p, OWN[c])
        sem = (0, c) if c < 2 else (16, 0)
        side_first.append(remote(qa.at[span], slot, sx.at[sem], rx.at[sem], side))
    for copy in side_first:
        copy.start()
    arrange(w, table_ref[384:896], qb, 8, 16)
    for c in range(2):
        b_start(b_own(c), b_relay(c), rr.at[c], cross_x)
        b_start(b_own(c), b_slot(src, c), rb.at[src, c], yup)
        b_start(b_own(c), b_slot(src, c), rb.at[src, c], ydown)
    for c in range(2):
        b_start(b_own(c), b_slot(src, c), rb.at[src, c], twin)
    local = [
        pltpu.make_async_copy(qa, a_all.at[z * 2 + p], loc.at[0]),
        pltpu.make_async_copy(qb, b_all.at[:, pl.ds(pl.multiple_of(src * 8, 8), 8)], loc.at[1]),
    ]
    for copy in local:
        copy.start()

    row = mask_ref[pl.ds(src, 1), :].astype(F32).astype(BF16)
    spread = lax.broadcasted_iota(jnp.int32, (16, 128), 1) // 8 == lax.broadcasted_iota(jnp.int32, (16, 128), 0)
    lanes = lax.broadcasted_iota(jnp.int32, (1, 128), 1)
    wt = jnp.dot(row, spread.astype(F32).astype(BF16), preferred_element_type=F32)
    wt = wt * jnp.where(lanes % 8 < 6, scale, 0.0)
    sign = jnp.where(lax.broadcasted_iota(jnp.int32, (8, 128), 0) < 4, 1.0, -1.0)
    wq = (wt * sign)[None]

    slot = units(z, col, OWN[2])
    remote(slot, slot, sx.at[16, 0], rx.at[16, 0], side).wait_recv()
    for c in range(2):
        for way in range(2):
            par(z, 0, way, c).start()

    last = ((0, 1), (2,)), ((0,), (1,))

    def step(t, final, between):
        zs = ((z + 16 - t) % 16, (z + t) % 16)
        for c in range(3):
            for way in range(2):
                own(zs[way], t - 1, way, c).wait_recv()
                if c in last[0][way]:
                    own(zs[way], t, way, c).start()
                elif final is None:
                    own(zs[way], t, way, c).start()
                else:
                    @pl.when(final)
                    def _():
                        own(zs[way], t, way, c).start()
                if c < 2:
                    side_send(zs[way], 2 * t - 1 + way, c).start()
            between(c)
        for c in range(2):
            for way in range(2):
                par(zs[way], t - 1, way, c).wait_recv()
                if c in last[1][way]:
                    par(zs[way], t, way, c).start()
                elif final is None:
                    par(zs[way], t, way, c).start()
                else:
                    @pl.when(final)
                    def _():
                        par(zs[way], t, way, c).start()
            between(3 + c)

    def b_events(t):
        def one(e):
            if (t, e) == (1, 2):
                for c in range(2):
                    remote(b_relay(c), b_relay(c), sb.at[0], rr.at[c], cross_x).wait_recv()
                    b_start(b_relay(c), b_slot(far_i, c), rb.at[far_i, c], side)
            if (t, e) == (1, 4):
                for d, c_on, peer in ((3, 0, yup), (1, 1, ydown)):
                    i = y_of(src, d)
                    for c in range(2):
                        b_wait(i, c)
                        if c == c_on:
                            b_pass(i, c, peer)
                        b_pass(i, c, twin)
            if (t, e) == (2, 2):
                for c in range(2):
                    b_wait(far_i, c)
                    b_pass(far_i, c, yup)
                    b_pass(far_i, c, ydown)
                    b_pass(far_i, c, twin)
            if (t, e) == (2, 4):
                for c in range(2):
                    b_wait(y_of(src, 2), c)
                    b_pass(y_of(src, 2), c, twin)
            if (t, e) == (3, 4):
                for d, c_on, peer in ((3, 0, yup), (1, 1, ydown)):
                    i = y_of(far_i, d)
                    for c in range(2):
                        b_wait(i, c)
                        if c == c_on:
                            b_pass(i, c, peer)
                        b_pass(i, c, twin)
            if (t, e) == (4, 2):
                for c in range(2):
                    b_wait(y_of(far_i, 2), c)
                    b_pass(y_of(far_i, 2), c, twin)
            if (t, e) == (4, 4):
                for base in (twin_i, (twin_i + 8) % 16):
                    for d in range(4):
                        for c in range(2):
                            b_wait((base // 8) * 8 + ((y + d) % 4) * 2 + 1 - low, c)

        return one

    for t in range(1, 5):
        step(t, None, b_events(t))
    for copy in local:
        copy.wait()
    for c in range(2):
        slot = units(z, col, SIDE[c])
        remote(slot, slot, sx.at[0, c], rx.at[0, c], side).wait_recv()

    def products(zs, lo, hi_):
        rows = 32 * len(zs)

        def body(fp, carry):
            keep = (lanes // 32 == fp % 4).astype(F32).astype(BF16)
            for h in range(2):
                f = fp + 16 * h
                lhs = jnp.concatenate(
                    [
                        jnp.concatenate(
                            [a_all[pl.ds(zz * 2, 2), u, 8 * h : 8 * h + 16, :].reshape(32, 128) for zz in zs], axis=0
                        )
                        for u in (fp, 16 + fp, 32 + fp // 4)
                    ],
                    axis=1,
                )
                rest = b_all[pl.ds(128 + 2 * (h * 4 + fp // 4), 2)].reshape(256, 128) * keep
                rhs = jnp.concatenate(
                    [
                        b_all[pl.ds(2 * f, 2)].reshape(256, 128),
                        b_all[pl.ds(64 + 2 * f, 2)].reshape(256, 128),
                        rest,
                    ],
                    axis=1,
                )
                r = lax.dot_general(lhs, rhs, NT, preferred_element_type=F32)
                pr = r[:, :128].reshape(rows // 8, 8, 128)
                qr = r[:, 128:].reshape(rows // 8, 8, 128)
                u = pr * wt[None] + pltpu.roll(qr, 4, 1) * wq
                u_ref[pl.ds(pl.multiple_of(f * 128, 128), rows), :] = u.reshape(rows, 128)
            return carry

        lax.fori_loop(lo, hi_, body, 0, unroll=UNROLL)

    sel = table_ref[896:992, 0:128]
    left = lax.broadcasted_iota(jnp.int32, (32, 128), 1) < 64

    def emit(zs, lo, hi_, unroll=1):
        def body(i4, carry):
            for part, zz in enumerate(zs):
                base = part * 32 + (i4 // 2) * 16 + i4 % 2
                rows = []
                for a in range(3):
                    for e in range(2):
                        r0 = (0, 2, 8)[a] + e * 4
                        r1 = (8, 10, 2)[a] + e * 4
                        rows.append(u_ref[pl.ds(base + r0, 16, stride=128), :])
                        rows.append(u_ref[pl.ds(16 * 128 + base + r1, 16, stride=128), :])
                xa = [jnp.concatenate(rows[4 * a : 4 * a + 4], axis=0).astype(BF16) for a in range(3)]
                rhs = jnp.concatenate([xa[0], xa[1], xa[1], xa[0], xa[2], xa[2]], axis=0)
                r = lax.dot_general(sel, rhs, NT, preferred_element_type=F32)
                t1, t2, t3 = r[:, :128], r[:, 128:256], r[:, 256:]
                b = lambda m, n: m[32 * n : 32 * n + 32]
                tiles = [
                    jnp.where(left, b(t1, 0), b(t2, 1)),
                    jnp.where(left, b(t1, 2), b(t1, 0)),
                    jnp.where(left, b(t2, 1), b(t1, 2)),
                    jnp.where(left, b(t3, 0), b(t3, 1)),
                    b(t3, 2)[:, :64],
                ]
                out_ref[zz * 4 + i4] = jnp.concatenate(tiles, axis=1).astype(BF16).reshape(16, 2, 576)
            return carry

        lax.fori_loop(lo, hi_, body, 0, unroll=unroll)

    def busy(t, carry):
        m = t - 5
        zs = [(z + 16 - 2 * m) % 16, (z + 2 * m + 1) % 16, (z + 15 - 2 * m) % 16, (z + 2 * m + 2) % 16]

        def between(e):
            if e == 0:
                for k in range(1, 5):
                    side_recv(4 * m + k)
                products(zs, 0, 4)
            if e == 1:
                products(zs, 4, 8)
            if e == 2:
                products(zs, 8, 16)
            if e == 3:
                emit(zs, 0, 2)
            if e == 4:
                emit(zs, 2, 4)

        step(t, t < 7, between)
        return carry

    lax.fori_loop(5, 8, busy, 0)
    side_recv(13)
    side_recv(14)
    z8 = (z + 8) % 16

    zs = [(z + 10) % 16, (z + 7) % 16, (z + 9) % 16]
    products(zs, 0, 16)
    for c in range(3):
        way = 0 if c in last[0][0] else 1
        own(z8, 7, way, c).wait_recv()
        if c < 2:
            side_send(z8, 15, c).start()
    emit(zs, 0, 4)
    for c in range(2):
        par(z8, 7, 0 if c in last[1][0] else 1, c).wait_recv()
    side_recv(15)
    products([z8], 0, 16)
    emit([z8], 0, 4, 4)

    def sent(t, carry):
        for way in range(2):
            for c in range(3):
                own(z, t, way, c).wait_send()
            for c in range(2):
                par(z, t, way, c).wait_send()
        return carry

    lax.fori_loop(0, 7, sent, 0)
    for way in range(2):
        for c in last[0][way]:
            own(z, 7, way, c).wait_send()
        for c in last[1][way]:
            par(z, 7, way, c).wait_send()
    for copy in side_first:
        copy.wait_send()

    def side_sent(k, carry):
        for c in range(2):
            side_send(z, k, c).wait_send()
        return carry

    lax.fori_loop(1, 16, side_sent, 0)
    for copy in b_sent:
        copy.wait_send()


def on_device(spectra, block_mask):
    count, segs, _ = spectra.shape
    last = np.pad(output_selector(), ((0, 0), (0, 256)))
    table = jnp.asarray(np.concatenate([source_selector(), receiver_selector(), last]), BF16)
    vmem = pl.BlockSpec(memory_space=pltpu.VMEM)
    dma = pltpu.SemaphoreType.DMA
    out = pl.pallas_call(
        functools.partial(fused, 1.0 / math.sqrt(segs)),
        out_shape=jax.ShapeDtypeStruct((64, 16, 2, 576), BF16),
        in_specs=[vmem] * 3,
        out_specs=vmem,
        scratch_shapes=[
            pltpu.VMEM((36, 24, 128), BF16),
            pltpu.VMEM((144, 8, 128), BF16),
            pltpu.VMEM((32, 36, 24, 128), BF16),
            pltpu.VMEM((144, 128, 128), BF16),
            pltpu.VMEM((144, 8, 128), BF16),
            pltpu.VMEM((32 * 128, 128), F32),
            dma((2, 8, 3)), dma((2, 8, 3)), dma((2, 8, 2)), dma((2, 8, 2)),
            dma((17, 2)), dma((17, 2)), dma((48,)), dma((16, 2)), dma((2,)), dma((2,)),
        ],
        compiler_params=pltpu.CompilerParams(
            collective_id=0, has_side_effects=True, vmem_limit_bytes=30 * 1024 * 1024
        ),
        name="fused",
    )(jnp.transpose(spectra, (1, 0, 2)), table, block_mask)
    return out


def solution(mesh):
    return jax.shard_map(
        on_device,
        mesh=mesh,
        in_specs=(P(("src", "rcv"), None, None), P()),
        out_specs=P("src", None, "rcv", None),
        check_vma=False,
    )
```
